32 devices in a mesh: section: 4 (over x, core), row: 4 (over z), col: 2 (over y).
Axes of the slice: x: 2, y: 2, z: 4, core: 2. Of those that a mesh axis runs over, the one named last changes fastest.
Arguments:
- frames: bfloat16 [3, 64, 64, 128], P(None, 'row', 'col'), may hold values from -6 to 6
- gate_weight: bfloat16 [4, 9, 256, 512], P('section'), may hold values from -0.16666667 to 0.16666667
- gate_bias: float32 [4, 512], P('section'), may hold values from -4 to 4
Outputs:
- hidden_final: bfloat16 [4, 64, 64, 128], P('section', 'row', 'col')
- cell_final: float32 [4, 64, 64, 128], P('section', 'row', 'col')
The draws below stay inside these ranges and needn't reach their ends.
All inputs are finite; a program needn't handle non-finite values.
Results may differ from the reference program's by a relative error of at most 0.0033.
Values may be sent and summed in bfloat16 or wider, within the bound.
A program may use at most 64 MiB of HBM per device.

```python
import jax
import jax.numpy as jnp

HID = 128
FRAMES = 3
LAYERS = 4
NR = 64
NC = 64


def draw_frames(key, part):
    whole_shape = (FRAMES, NR, NC, HID)
    grid_rows = jnp.arange(NR)[:, None]
    grid_cols = jnp.arange(NC)[None, :]
    checker = 1.0 - 2.0 * ((grid_rows + grid_cols) % 2).astype(jnp.float32)
    magnitude = jnp.minimum(jnp.abs(jax.random.normal(key, whole_shape, jnp.float32)), 6.0)
    return (magnitude * checker[None, :, :, None]).astype(jnp.bfloat16)


def draw_gate_weight(key, part):
    whole_shape = (LAYERS, 9, 2 * HID, 4 * HID)
    base_scale = (18.0 * HID) ** (-0.5)
    factors = jnp.array([4.0, 1.0, 4.0, 1.0, 0.5, 1.0, 4.0, 1.0, 4.0], jnp.float32) * base_scale
    values = jax.random.normal(key, whole_shape, jnp.float32)
    scaled = values * factors[None, :, None, None]
    limit = 7.96 * base_scale
    return jnp.clip(scaled, -limit, limit).astype(jnp.bfloat16)


def levels(stream_key, dims, cuts, least, largest):
    loudness = 1.0
    for dim, blocks in cuts:
        heights = jax.random.uniform(jax.random.fold_in(jax.random.fold_in(stream_key, 6), dim), (blocks,), jnp.float32, least / len(cuts), largest / len(cuts))
        loudness = loudness * jnp.repeat(jnp.exp(heights), dims[dim] // blocks).reshape((-1,) + (1,) * (len(dims) - 1 - dim))
    return loudness


def gaussian(rng, dims, spread, reach, shards=(), dtype=jnp.bfloat16):
    values = jax.random.normal(rng, dims, jnp.float32) * spread
    if len(shards) > 0:
        values = levels(rng, dims, shards, -0.22, 0.18) * values
    return jnp.clip(values, min=-reach, max=reach).astype(dtype)


def setup_inputs(seed: int = 0) -> dict:
    arg_keys = jax.random.split(jax.random.key(seed), 4)
    frames = draw_frames(jax.random.fold_in(arg_keys[3], 71), 0)
    gate_weight = draw_gate_weight(jax.random.fold_in(arg_keys[3], 71), 0)
    gate_bias = gaussian(arg_keys[2], (LAYERS, 4 * HID), 1.0, 4.0, ((0, 4),), jnp.float32)
    return dict(frames=frames, gate_weight=gate_weight, gate_bias=gate_bias)


def convolve(stack, kernel, bias):
    rows, cols = stack.shape[0], stack.shape[1]
    padded = jnp.pad(stack, ((1, 1), (1, 1), (0, 0)))
    total = jnp.zeros((rows * cols, kernel.shape[-1]), jnp.float32) + bias
    for offset in range(9):
        drow, dcol = offset // 3, offset % 3
        window = padded[drow:drow + rows, dcol:dcol + cols].reshape(rows * cols, -1)
        total = total + jnp.dot(window, kernel[offset], preferred_element_type=jnp.float32)
    return total.reshape(rows, cols, -1)


def reference(frames, gate_weight, gate_bias):
    nlayer = gate_weight.shape[0]
    width = frames.shape[-1]
    inputs = [frames[t] for t in range(frames.shape[0])]
    hiddens = []
    cells = []
    for layer in range(nlayer):
        hidden = jnp.zeros(frames.shape[1:], jnp.bfloat16)
        cell = jnp.zeros(frames.shape[1:], jnp.float32)
        outputs = []
        for t in range(len(inputs)):
            stack = jnp.concatenate([inputs[t], hidden], axis=-1)
            pre = convolve(stack, gate_weight[layer], gate_bias[layer])
            gate_in = pre[..., :width]
            forget = pre[..., width:2 * width]
            candidate = pre[..., 2 * width:3 * width]
            gate_out = pre[..., 3 * width:]
            cell = jax.nn.sigmoid(forget) * cell + jax.nn.sigmoid(gate_in) * jnp.tanh(candidate)
            hidden = (jax.nn.sigmoid(gate_out) * jnp.tanh(cell)).astype(jnp.bfloat16)
            outputs.append(hidden)
        inputs = outputs
        hiddens.append(hidden)
        cells.append(cell)
    return jnp.stack(hiddens), jnp.stack(cells)
```

```python
import jax
import jax.numpy as jnp
from jax import lax
from jax.experimental import pallas as pl
from jax.experimental.pallas import tpu as pltpu
from jax.sharding import PartitionSpec as P

MESH = pl.DeviceIdType.MESH
DIRS = [(dr, dc) for dr in (-1, 0, 1) for dc in (-1, 0, 1) if (dr, dc) != (0, 0)]
SIDE = 8
CHUNK = 6


def sigmoid(v):
    return 0.5 * jnp.tanh(0.5 * v) + 0.5


def slot(dr, dc):
    return (dr + 1) * 3 + (dc + 1)


def body(sizes, frames, weight, bias, kept_out, added_out, gate_out,
         xc, xe, hc, col_x, col_h, w, ax, ah, acc, cell_mem,
         local_sem, send_sem, xrecv):
    nsec, nrow, ncol = sizes
    steps, rows, cols, width = frames.shape
    pad = steps
    wide = cols + 2 * SIDE
    sec, row, col = lax.axis_index("section"), lax.axis_index("row"), lax.axis_index("col")

    def load_frame(t):
        return pltpu.make_async_copy(frames.at[t], xc.at[t, pl.ds(pad, rows)], local_sem.at[t])

    load_w = pltpu.make_async_copy(weight.at[0], w, local_sem.at[steps])

    @pl.when(sec == 0)
    def _():
        for t in range(steps):
            load_frame(t).start()

    load_w.start()

    def there(dr, dc):
        ok = sec >= 0
        if dr:
            ok = (row > 0) if dr < 0 else (row < nrow - 1)
        if dc:
            okc = (col > 0) if dc < 0 else (col < ncol - 1)
            ok = jnp.logical_and(ok, okc) if dr else okc
        return ok

    def device(ds, dr, dc):
        return {"section": sec + ds, "row": row + dr, "col": col + dc}

    barrier = pltpu.get_barrier_semaphore()

    for t in range(steps):
        xc[t, 0:pad] = jnp.zeros((pad, cols, width), jnp.bfloat16)
        xc[t, pad + rows:] = jnp.zeros((pad, cols, width), jnp.bfloat16)
        xe[t] = jnp.zeros(xe.shape[1:], jnp.bfloat16)

    for ds in (-1, 0, 1):
        okd = (sec > 0) if ds < 0 else (sec < nsec - 1) if ds > 0 else (sec == 0)
        for dr, dc in [(0, 0)] + DIRS:
            if ds == 0 and (dr, dc) == (0, 0):
                continue

            @pl.when(jnp.logical_and(there(dr, dc), okd))
            def _(ds=ds, dr=dr, dc=dc):
                pl.semaphore_signal(barrier, inc=1, device_id=device(ds, dr, dc), device_id_type=MESH)

    def extent(pos, count):
        return 1 + jnp.where(pos > 0, 1, 0) + jnp.where(pos < count - 1, 1, 0)

    near = extent(row, nrow) * extent(col, ncol)
    pl.semaphore_wait(barrier, (extent(sec, nsec) - 1) * near + jnp.where(sec == 0, near - 1, 0))

    def halo_copy(center, base, colbuf, t, kind, ds, dr, dc):
        reach = steps - t
        if dr == 0:
            mine, theirs = pl.ds(0, rows), pl.ds(pad, rows)
        elif dr < 0:
            mine, theirs = pl.ds(0, reach), pl.ds(pad + rows, reach)
        else:
            mine, theirs = pl.ds(rows - reach, reach), pl.ds(pad - reach, reach)
        if dc == 0:
            src = center.at[t, pl.ds(base + (rows - reach if dr > 0 else 0), reach)]
            dst = xc.at[t, theirs]
        else:
            src = colbuf.at[t, 1 if dc > 0 else 0, mine]
            dst = xe.at[t, 0 if dc > 0 else 1, theirs]
        return pltpu.make_async_remote_copy(
            src_ref=src, dst_ref=dst,
            send_sem=send_sem.at[t, kind, slot(dr, dc)],
            recv_sem=xrecv.at[t, slot(-dr, -dc)],
            device_id=device(ds, dr, dc), device_id_type=MESH,
        )

    def halo_sends(act, center, base, colbuf, t, kind, ds):
        for dr, dc in sorted(DIRS, key=lambda d: -abs(d[0]) - abs(d[1])):
            @pl.when(there(dr, dc))
            def _(dr=dr, dc=dc):
                copy = halo_copy(center, base, colbuf, t, kind, ds, dr, dc)
                copy.start() if act == "start" else copy.wait_send()

    def halo_waits(t):
        reach = steps - t
        for dr, dc in DIRS:
            @pl.when(there(dr, dc))
            def _(dr=dr, dc=dc):
                mine = pl.ds(pad, rows) if dr == 0 else pl.ds(pad - reach if dr < 0 else pad + rows, reach)
                dst = xc.at[t, mine] if dc == 0 else xe.at[t, 0 if dc < 0 else 1, mine]
                pltpu.make_async_remote_copy(
                    src_ref=dst, dst_ref=dst,
                    send_sem=send_sem.at[t, 0, slot(0, 0)],
                    recv_sem=xrecv.at[t, slot(dr, dc)],
                    device_id=device(0, dr, dc), device_id_type=MESH,
                ).wait_recv()

    def center_copy(t):
        return pltpu.make_async_remote_copy(
            src_ref=hc.at[t], dst_ref=xc.at[t, pl.ds(pad, rows)],
            send_sem=send_sem.at[t, 0, slot(0, 0)], recv_sem=xrecv.at[t, slot(0, 0)],
            device_id=device(1, 0, 0), device_id_type=MESH,
        )

    @pl.when(sec == 0)
    def _():
        for t in range(steps):
            load_frame(t).wait()
            value = xc[t, pad:pad + rows].astype(jnp.float32)
            col_x[t, 0] = value[:, :SIDE].astype(jnp.bfloat16)
            col_x[t, 1] = value[:, cols - SIDE:].astype(jnp.bfloat16)
            halo_sends("start", xc, pad, col_x, t, 1, 0)

    place = lax.broadcasted_iota(jnp.int32, (wide, width), 0)
    left = jnp.where(col > 0, 1.0, 0.0)
    right = jnp.where(col < ncol - 1, 1.0, 0.0)
    inside = jnp.where(place < SIDE, left, jnp.where(place >= SIDE + cols, right, 1.0))
    above = jnp.where(row > 0, 1.0, 0.0)
    below = jnp.where(row < nrow - 1, 1.0, 0.0)

    def put(out, r, line, full):
        shifted = [pltpu.roll(line, 1, 0), line, pltpu.roll(line, wide - 1, 0)]
        for k, v in enumerate(shifted):
            v = v if full else v[SIDE:SIDE + cols]
            out[r, 0:v.shape[0], k * width:(k + 1) * width] = v.astype(jnp.bfloat16)

    def patches(a, first, count, span):
        return jnp.concatenate(
            [a[first + k:first + k + count, 0:span].reshape(count * span, 3 * width) for k in (-1, 0, 1)], axis=-1
        )

    def kernel_of(half):
        return w[:, half * width:(half + 1) * width, :].reshape(9 * width, 4 * width)

    for t in range(steps):
        e = steps - 1 - t
        full = t < steps - 1
        span = wide if full else cols
        first, last = pad - e, pad + rows + e
        total = (last - first) * span
        if t > 0:
            acc[0:total] = jnp.dot(patches(ah, first, last - first, span), kernel_of(1),
                                   preferred_element_type=jnp.float32)

        @pl.when(sec > 0)
        def _(t=t):
            center = xc.at[t, pl.ds(pad, rows)]
            pltpu.make_async_remote_copy(
                src_ref=center, dst_ref=center, send_sem=send_sem.at[t, 0, slot(0, 0)],
                recv_sem=xrecv.at[t, slot(0, 0)], device_id=device(-1, 0, 0), device_id_type=MESH,
            ).wait_recv()

        halo_waits(t)
        for r in range(first - 1, last + 1):
            line = jnp.concatenate([v.astype(jnp.float32) for v in (xe[t, 0, r], xc[t, r], xe[t, 1, r])], axis=0)
            put(ax, r, line, full)
        if t == 0:
            load_w.wait()
        for r in range(first, last, CHUNK):
            count = min(CHUNK, last - r)
            at = (r - first) * span
            pre = jnp.dot(patches(ax, r, count, span), kernel_of(0), preferred_element_type=jnp.float32)
            pre = pre + bias[...]
            if t > 0:
                pre = pre + acc[at:at + count * span]
            added = sigmoid(pre[:, :width]) * jnp.tanh(pre[:, 2 * width:3 * width])
            added = added.reshape(count, span, width)
            cell = added
            if t > 0:
                old = cell_mem[r:r + count]
                old = old if full else old[:, SIDE:SIDE + cols]
                kept = sigmoid(pre[:, width:2 * width]).reshape(count, span, width) * old
                cell = kept + added
            opened = sigmoid(pre[:, 3 * width:]).reshape(count, span, width)
            hidden = opened * jnp.tanh(cell)
            if full:
                cell_mem[r:r + count] = cell
            else:
                kept_out[0, r - pad:r - pad + count] = kept
                added_out[0, r - pad:r - pad + count] = added
                gate_out[0, r - pad:r - pad + count] = opened
            for q in range(r, r + count):
                line = hidden[q - r]
                core = line[SIDE:SIDE + cols] if full else line
                if pad <= q < pad + rows:
                    hc[t, q - pad] = core.astype(jnp.bfloat16)
                    col_h[t, 0, q - pad] = core[:SIDE].astype(jnp.bfloat16)
                    col_h[t, 1, q - pad] = core[cols - SIDE:].astype(jnp.bfloat16)
                if full:
                    line = line * inside
                    line = line * above if q < pad else line * below if q >= pad + rows else line
                    put(ah, q, line, t + 1 < steps - 1)

        @pl.when(sec < nsec - 1)
        def _(t=t):
            halo_sends("start", hc, 0, col_h, t, 0, 1)
            center_copy(t).start()

    @pl.when(sec == 0)
    def _():
        for t in range(steps):
            halo_sends("wait", xc, pad, col_x, t, 1, 0)

    @pl.when(sec < nsec - 1)
    def _():
        for t in range(steps):
            center_copy(t).wait_send()
            halo_sends("wait", hc, 0, col_h, t, 0, 1)


def solution(mesh):
    sizes = (mesh.shape["section"], mesh.shape["row"], mesh.shape["col"])

    def step(frames, weight, bias):
        steps, rows, cols, width = frames.shape
        high, wide = rows + 2 * steps, cols + 2 * SIDE
        vmem = pl.BlockSpec(memory_space=pltpu.VMEM)
        hbm = pl.BlockSpec(memory_space=pltpu.HBM)
        bf16 = jnp.bfloat16
        kept, added, opened = pl.pallas_call(
            lambda *refs: body(sizes, *refs),
            out_shape=(jax.ShapeDtypeStruct((1, rows, cols, width), jnp.float32),) * 3,
            in_specs=[hbm, hbm, vmem],
            out_specs=(vmem, vmem, vmem),
            scratch_shapes=[
                pltpu.VMEM((steps, high, cols, width), bf16),
                pltpu.VMEM((steps, 2, high, SIDE, width), bf16),
                pltpu.VMEM((steps, rows, cols, width), bf16),
                pltpu.VMEM((steps, 2, rows, SIDE, width), bf16),
                pltpu.VMEM((steps, 2, rows, SIDE, width), bf16),
                pltpu.VMEM(weight.shape[1:], bf16),
                pltpu.VMEM((high, wide, 3 * width), bf16),
                pltpu.VMEM((high, wide, 3 * width), bf16),
                pltpu.VMEM((high * wide, 4 * width), jnp.float32),
                pltpu.VMEM((high, wide, width), jnp.float32),
                pltpu.SemaphoreType.DMA((steps + 1,)),
                pltpu.SemaphoreType.DMA((steps, 2, 9)),
                pltpu.SemaphoreType.DMA((steps, 9)),
            ],
            compiler_params=pltpu.CompilerParams(collective_id=0, has_side_effects=True, vmem_limit_bytes=20<<20),
        )(*[pltpu.with_memory_space_constraint(v, pltpu.HBM) for v in (frames, weight, bias)])
        cell = kept + added
        return (opened * jnp.tanh(cell)).astype(bf16), cell

    return jax.shard_map(
        step,
        mesh=mesh,
        in_specs=(P(None, "row", "col", None), P("section", None, None, None), P("section", None)),
        out_specs=(P("section", "row", "col", None), P("section", "row", "col", None)),
        check_vma=False,
    )
```

```python
import jax
import jax.numpy as jnp
from jax import lax
from jax.experimental import pallas as pl
from jax.experimental.pallas import tpu as pltpu
from jax.sharding import PartitionSpec as P

MESH = pl.DeviceIdType.MESH
DIRS = [(dr, dc) for dr in (-1, 0, 1) for dc in (-1, 0, 1) if (dr, dc) != (0, 0)]
RING = 8
MSGS = 15


def sigmoid(v):
    return 0.5 * jnp.tanh(0.5 * v) + 0.5


def body(sizes, frames, weight, bias_in, kept_out, added_out, gate_out,
         xc, xe, hc, hr, col_h, w, bias, sx, rx, sh, rh, acc, cell_c, cell_r,
         local_sem, frame_sem, send_sem, recv_sem):
    nsec, nrow, ncol = sizes
    steps, rows, cols, width = frames.shape
    pad = steps + 1
    wide = cols + RING
    bf16 = jnp.bfloat16
    f32 = jnp.float32
    sec, row, col = lax.axis_index("section"), lax.axis_index("row"), lax.axis_index("col")

    def there(dr, dc):
        ok = sec >= 0
        if dr:
            ok = (row > 0) if dr < 0 else (row < nrow - 1)
        if dc:
            okc = (col > 0) if dc < 0 else (col < ncol - 1)
            ok = jnp.logical_and(ok, okc) if dr else okc
        return ok

    def device(ds, dr, dc):
        return {"section": sec + ds, "row": row + dr, "col": col + dc}

    def load_frame(t):
        return pltpu.make_async_copy(frames.at[t], xc.at[t, pl.ds(pad, rows)], local_sem.at[t])

    def load_w(half):
        part = pl.ds(half * width, width)
        return pltpu.make_async_copy(weight.at[0, :, part], w.at[:, part], local_sem.at[steps + half])

    load_b = pltpu.make_async_copy(bias_in, bias, local_sem.at[steps + 2])

    def direct(s):
        return s % 2 == 0

    def extra(s, t):
        return steps - t - s % 2

    def edge(s):
        return nsec + 1 - s

    def rng(a, b):
        return pl.ds(pad + a, b - a)

    def halo(t, reach, dr, dc):
        if dr == 0:
            return (0, rows), (0, rows)
        if dr < 0:
            return (0, reach), (rows, rows + reach)
        return (rows - reach, rows), (-reach, 0)

    def frame_msgs(t):
        reach = pad - t
        out = []
        for dr, dc in sorted(DIRS, key=lambda d: -abs(d[0]) - abs(d[1])):
            mine, theirs = halo(t, reach, dr, dc)
            src = frames.at[t, pl.ds(mine[0], mine[1] - mine[0])]
            if dc == 0:
                dst = xc.at[t, rng(*theirs)]
            else:
                src = frames.at[t, pl.ds(mine[0], mine[1] - mine[0]), pl.ds(0 if dc < 0 else cols - RING, RING)]
                dst = xe.at[t, 1 if dc < 0 else 0, rng(*theirs)]
            out.append((dr, dc, src, dst, 3 * (dr + 1) + dc + 1))
        return out

    def exchange_msgs(s, t, phase):
        reach, q = pad - t, edge(s)
        out = []

        def side(dc, mine, theirs, k, dr=0):
            src = col_h.at[t, 0 if dc < 0 else 1, pl.ds(mine[0], mine[1] - mine[0])]
            dst = xe.at[t, 1 if dc < 0 else 0, rng(*theirs)]
            out.append((dr, dc, src, dst, k))

        def middle(mine, theirs, k, dr=0):
            out.append((dr, 0, hc.at[t, rng(*mine)], xc.at[t, rng(*theirs)], k))

        if phase == 0:
            for k, (dr, dc) in enumerate([d for d in DIRS if d[0] and d[1]]):
                mine, theirs = halo(t, reach, dr, dc)
                side(dc, mine, theirs, 8 + k, dr)
            for k, dr in enumerate((-1, 1)):
                mine, theirs = halo(t, reach, dr, 0)
                middle(mine, theirs, 2 + k, dr)
            for k, span in enumerate(((0, q), (rows - q, rows))):
                for j, dc in enumerate((-1, 1)):
                    side(dc, span, span, 4 + 2 * j + k)
            for k, span in enumerate(((0, q), (rows - q, rows))):
                middle(span, span, k)
        else:
            span = (q, rows - q)
            for j, dc in enumerate((-1, 1)):
                side(dc, span, span, 13 + j)
            middle(span, span, 12)
        return out

    def direct_msgs(s, t, phase):
        e, q = extra(s, t), edge(s)
        spans = ((-e, q), (rows - q, rows + e)) if phase == 0 else ((q, rows - q),)
        out = []
        for k, span in enumerate(spans):
            at = rng(*span)
            out.append((0, 0, hc.at[t, at], xc.at[t, at], 6 * phase + 2 * k))
            out.append((0, 0, hr.at[t, at], xe.at[t, 0, at], 6 * phase + 2 * k + 1))
        return out

    def msgs(s, t, phase):
        return direct_msgs(s, t, phase) if direct(s) else exchange_msgs(s, t, phase)

    def each(items, ds, t, sem, act):
        for dr, dc, src, dst, k in items:
            def go(dr=dr, dc=dc, src=src, dst=dst, k=k):
                if act == "recv":
                    pltpu.make_async_remote_copy(
                        src_ref=dst, dst_ref=dst, send_sem=sem.at[t, k], recv_sem=recv_sem.at[t, k],
                        device_id=device(-ds, -dr, -dc), device_id_type=MESH,
                    ).wait_recv()
                    return
                copy = pltpu.make_async_remote_copy(
                    src_ref=src, dst_ref=dst, send_sem=sem.at[t, k], recv_sem=recv_sem.at[t, k],
                    device_id=device(ds, dr, dc), device_id_type=MESH,
                )
                copy.start() if act == "start" else copy.wait_send()
            if (dr, dc) == (0, 0):
                go()
            else:
                pl.when(there(-dr, -dc) if act == "recv" else there(dr, dc))(go)

    barrier = pltpu.get_barrier_semaphore()

    def signal(ds, dr, dc):
        def go():
            pl.semaphore_signal(barrier, inc=1, device_id=device(ds, dr, dc), device_id_type=MESH)
        if (dr, dc) == (0, 0):
            go()
        else:
            pl.when(there(dr, dc))(go)

    def extent(pos, count):
        return 1 + jnp.where(pos > 0, 1, 0) + jnp.where(pos < count - 1, 1, 0)

    near = extent(row, nrow) * extent(col, ncol)

    place = lax.broadcasted_iota(jnp.int32, (RING, width), 0)
    left = jnp.where(col > 0, 1.0, 0.0)
    right = jnp.where(col < ncol - 1, 1.0, 0.0)
    inside = jnp.where(place < RING // 2, right, left)
    above = jnp.where(row > 0, 1.0, 0.0)
    below = jnp.where(row < nrow - 1, 1.0, 0.0)

    def spread(shift, ring, r, line):
        back, ahead = pltpu.roll(line, 1, 0), pltpu.roll(line, wide - 1, 0)
        shift[r + pad, :, 0:width] = back[:cols].astype(bf16)
        shift[r + pad, :, width:] = ahead[:cols].astype(bf16)
        for k, v in enumerate((back, line, ahead)):
            ring[(r + pad) * RING:(r + pad + 1) * RING, k * width:(k + 1) * width] = v[cols:]

    def taps(center, shift, ring, pieces, has_ring, which):
        blocks = []
        for k in which:
            dr, dc = k // 3 - 1, k % 3 - 1
            parts = []
            for r0, n in pieces:
                at = slice(r0 + dr + pad, r0 + dr + pad + n)
                v = center[at] if dc == 0 else shift[at, :, 0:width] if dc < 0 else shift[at, :, width:]
                parts.append(v.reshape(n * cols, width))
            if has_ring:
                lines = [ring[(r0 + dr + pad) * RING:(r0 + dr + pad + n) * RING, (dc + 1) * width:(dc + 2) * width]
                         for r0, n in pieces]
                parts.append((jnp.concatenate(lines, axis=0) if len(lines) > 1 else lines[0]).astype(bf16))
            blocks.append(jnp.concatenate(parts, axis=0) if len(parts) > 1 else parts[0])
        return blocks

    def kernel_of(half, which):
        return [w[k, half * width:(half + 1) * width, :] for k in which]

    def dot(a, b):
        return jnp.dot(jnp.concatenate(a, axis=1), jnp.concatenate(b, axis=0), preferred_element_type=f32)

    every = list(range(9))

    def section(s):
        last_sec = s == nsec - 1
        q = edge(s)

        load_w(0).start()
        load_b.start()
        load_w(1).start()
        if s == 0:
            for t in range(steps):
                load_frame(t).start()
        if direct(s):
            for t in range(steps):
                xc[t, 0:pad] = jnp.zeros((pad, cols, width), bf16)
                xc[t, pad + rows:] = jnp.zeros((pad, cols, width), bf16)
                xe[t] = jnp.zeros(xe.shape[1:], bf16)
        if s == 0:
            for dr, dc in DIRS:
                signal(0, dr, dc)
        elif direct(s - 1):
            signal(-1, 0, 0)
        else:
            for dr, dc in [(0, 0)] + DIRS:
                signal(-1, dr, dc)
        wanted = 0
        if s == 0:
            wanted = near - 1
        if not last_sec:
            wanted = wanted + (1 if direct(s) else near)
        if s == 0 or not last_sec:
            pl.semaphore_wait(barrier, wanted)
        if s == 0:
            for t in range(steps):
                each(frame_msgs(t), 0, t, frame_sem, "start")

        for t in range(steps):
            e = extra(s, t)
            has_ring = e > 0
            span = wide if has_ring else cols
            final = t == steps - 1
            chunks = [[(-e, q + e), (rows - q, q + e)], [(q, rows - 2 * q)]]
            fresh = [[(-e - 1, q + 1), (rows - q - 1, rows + e + 1)], [(q + 1, rows - q - 1)]]
            sizes_m = [sum(n for _, n in c) * span for c in chunks]
            starts = [0, sizes_m[0]]
            if t > 0:
                if t == 1:
                    load_w(1).wait()
                if s > 0:
                    for c in range(2):
                        acc[starts[c]:starts[c] + sizes_m[c]] = dot(
                            taps(hc.at[t - 1], sh.at[t - 1], rh.at[t - 1], chunks[c], has_ring, every[:8]),
                            kernel_of(1, every[:8]))
            for c in range(2):
                pieces = chunks[c]
                if s > 0:
                    each(msgs(s - 1, t, c), 1, t, send_sem, "recv")
                elif c == 0:
                    load_frame(t).wait()
                    each(frame_msgs(t), 0, t, frame_sem, "recv")
                for lo, hi in fresh[c]:
                    for r in range(lo, hi):
                        if direct(s):
                            ring = jnp.where(place < RING // 2, xe[t, 1, r + pad].astype(f32), xe[t, 0, r + pad].astype(f32))
                        else:
                            ring = xe[t, 0, r + pad].astype(f32)
                        spread(sx, rx, r, jnp.concatenate([xc[t, r + pad].astype(f32), ring], axis=0))
                if t == 0 and c == 0:
                    load_w(0).wait()
                    load_b.wait()
                a = taps(xc.at[t], sx, rx, pieces, has_ring, every)
                b = kernel_of(0, every)
                if t > 0:
                    which = every if s == 0 else every[8:]
                    a = a + taps(hc.at[t - 1], sh.at[t - 1], rh.at[t - 1], pieces, has_ring, which)
                    b = b + kernel_of(1, which)
                pre = dot(a, b) + bias[...]
                if t > 0 and s > 0:
                    pre = pre + acc[starts[c]:starts[c] + sizes_m[c]]
                total = sum(n for _, n in pieces)
                at_core, at_ring = 0, total * cols
                for r0, n in pieces:
                    groups = [(cols, at_core, cell_c)] + ([(RING, at_ring, cell_r)] if has_ring else [])
                    made = []
                    for span_g, at, mem in groups:
                        p = pre[at:at + n * span_g]
                        shape = (n, span_g, width)
                        added = (sigmoid(p[:, :width]) * jnp.tanh(p[:, 2 * width:3 * width])).reshape(shape)
                        cell = added
                        if t > 0:
                            kept = sigmoid(p[:, width:2 * width]).reshape(shape) * mem[r0 + pad:r0 + pad + n]
                            cell = kept + added
                        opened = sigmoid(p[:, 3 * width:]).reshape(shape)
                        if not final:
                            mem[r0 + pad:r0 + pad + n] = cell
                        elif span_g == cols:
                            lo, hi = max(r0, 0), min(r0 + n, rows)
                            kept_out[0, lo:hi] = kept[lo - r0:hi - r0]
                            added_out[0, lo:hi] = added[lo - r0:hi - r0]
                            gate_out[0, lo:hi] = opened[lo - r0:hi - r0]
                        made.append(opened * jnp.tanh(cell))
                    at_core, at_ring = at_core + n * cols, at_ring + n * RING
                    if final and last_sec:
                        continue
                    for r in range(r0, r0 + n):
                        core = made[0][r - r0]
                        if has_ring:
                            ring = made[1][r - r0] * inside
                        if r < 0:
                            core, ring = core * above, ring * above
                        elif r >= rows:
                            core, ring = core * below, ring * below
                        hc[t, r + pad] = core.astype(bf16)
                        if not last_sec:
                            if direct(s):
                                hr[t, r + pad] = ring.astype(bf16)
                            elif 0 <= r < rows:
                                col_h[t, 0, r] = core[:RING].astype(bf16)
                                col_h[t, 1, r] = core[cols - RING:].astype(bf16)
                        if not final:
                            spread(sh.at[t], rh.at[t], r, jnp.concatenate([core, ring], axis=0))
                if not last_sec:
                    each(msgs(s, t, c), 1, t, send_sem, "start")

        if s == 0:
            for t in range(steps):
                each(frame_msgs(t), 0, t, frame_sem, "wait")
        if steps == 1:
            load_w(1).wait()
        if not last_sec:
            for t in range(steps):
                for c in range(2):
                    each(msgs(s, t, c), 1, t, send_sem, "wait")

    for s in range(nsec):
        @pl.when(sec == s)
        def _(s=s):
            section(s)


def solution(mesh):
    sizes = (mesh.shape["section"], mesh.shape["row"], mesh.shape["col"])

    def step(frames, weight, bias):
        steps, rows, cols, width = frames.shape
        pad = steps + 1
        assert pad <= RING // 2 and 2 * (sizes[0] + 1) < rows
        high = rows + 2 * pad
        vmem = pl.BlockSpec(memory_space=pltpu.VMEM)
        hbm = pl.BlockSpec(memory_space=pl.ANY)
        bf16, f32 = jnp.bfloat16, jnp.float32
        kept, added, opened = pl.pallas_call(
            lambda *refs: body(sizes, *refs),
            out_shape=(jax.ShapeDtypeStruct((1, rows, cols, width), f32),) * 3,
            in_specs=[hbm, hbm, hbm],
            out_specs=(vmem, vmem, vmem),
            scratch_shapes=[
                pltpu.VMEM((steps, high, cols, width), bf16),
                pltpu.VMEM((steps, 2, high, RING, width), bf16),
                pltpu.VMEM((steps, high, cols, width), bf16),
                pltpu.VMEM((steps, high, RING, width), bf16),
                pltpu.VMEM((steps, 2, rows, RING, width), bf16),
                pltpu.VMEM(weight.shape[1:], bf16),
                pltpu.VMEM(bias.shape, f32),
                pltpu.VMEM((high, cols, 2 * width), bf16),
                pltpu.VMEM((high * RING, 3 * width), f32),
                pltpu.VMEM((steps, high, cols, 2 * width), bf16),
                pltpu.VMEM((steps, high * RING, 3 * width), f32),
                pltpu.VMEM((high * (cols + RING), 4 * width), f32),
                pltpu.VMEM((high, cols, width), f32),
                pltpu.VMEM((high, RING, width), f32),
                pltpu.SemaphoreType.DMA((steps + 3,)),
                pltpu.SemaphoreType.DMA((steps, MSGS)),
                pltpu.SemaphoreType.DMA((steps, MSGS)),
                pltpu.SemaphoreType.DMA((steps, MSGS)),
            ],
            compiler_params=pltpu.CompilerParams(
                collective_id=0, has_side_effects=True, vmem_limit_bytes=24 << 20),
        )(*[pltpu.with_memory_space_constraint(v, pltpu.HBM) for v in (frames, weight, bias)])
        cell = kept + added
        return (opened * jnp.tanh(cell)).astype(bf16), cell

    return jax.shard_map(
        step,
        mesh=mesh,
        in_specs=(P(None, "row", "col", None), P("section", None, None, None), P("section", None)),
        out_specs=(P("section", "row", "col", None), P("section", "row", "col", None)),
        check_vma=False,
    )
```

```python
import jax
import jax.numpy as jnp
from jax import lax
from jax.experimental import pallas as pl
from jax.experimental.pallas import tpu as pltpu
from jax.sharding import PartitionSpec as P

MESH = pl.DeviceIdType.MESH
DIRS = [(dr, dc) for dr in (-1, 0, 1) for dc in (-1, 0, 1) if (dr, dc) != (0, 0)]
RING = 8
MSGS = 15


def sigmoid(v):
    return 0.5 * jnp.tanh(0.5 * v) + 0.5


def body(sizes, frames, weight, bias_in, kept_out, added_out, gate_out,
         xc, xe, xn, hc, hr, col_h, col_n, w, bias, sx, rx, sh, rh, acc, cell_c, cell_r,
         local_sem, frame_sem, send_sem, recv_sem):
    nsec, nrow, ncol = sizes
    steps, rows, cols, width = frames.shape
    pad = steps + 1
    wide = cols + RING
    bf16 = jnp.bfloat16
    f32 = jnp.float32
    sec, row, col = lax.axis_index("section"), lax.axis_index("row"), lax.axis_index("col")

    def there(dr, dc):
        ok = sec >= 0
        if dr:
            ok = (row > 0) if dr < 0 else (row < nrow - 1)
        if dc:
            okc = (col > 0) if dc < 0 else (col < ncol - 1)
            ok = jnp.logical_and(ok, okc) if dr else okc
        return ok

    def device(ds, dr, dc):
        return {"section": sec + ds, "row": row + dr, "col": col + dc}

    def load_frame(t):
        return pltpu.make_async_copy(frames.at[t], xc.at[t, pl.ds(pad, rows)], local_sem.at[t])

    def load_side(t, k):
        part = pl.ds(0 if k == 0 else cols - RING, RING)
        return pltpu.make_async_copy(frames.at[t, :, part], col_h.at[t, k], local_sem.at[steps + 3 + 2 * t + k])

    def load_w(half):
        part = pl.ds(half * width, width)
        return pltpu.make_async_copy(weight.at[0, :, part], w.at[:, part], local_sem.at[steps + half])

    load_b = pltpu.make_async_copy(bias_in, bias, local_sem.at[steps + 2])

    def direct(s):
        return s % 2 == 0

    def extra(s, t):
        return steps - t - s % 2

    def edge(s):
        return nsec + 1 - s

    def rng(a, b):
        return pl.ds(pad + a, b - a)

    def halo(t, reach, dr, dc):
        if dr == 0:
            return (0, rows), (0, rows)
        if dr < 0:
            return (0, reach), (rows, rows + reach)
        return (rows - reach, rows), (-reach, 0)

    def frame_msgs(t):
        reach = pad - t
        out = []
        for dr, dc in sorted(DIRS, key=lambda d: -abs(d[0]) - abs(d[1])):
            mine, theirs = halo(t, reach, dr, dc)
            if dc == 0:
                src = xc.at[t, rng(*mine)]
                dst = xc.at[t, rng(*theirs)]
            else:
                src = col_h.at[t, 0 if dc < 0 else 1, pl.ds(mine[0], mine[1] - mine[0])]
                dst = xe.at[t, 1 if dc < 0 else 0, rng(*theirs)]
            out.append((dr, dc, src, dst, 3 * (dr + 1) + dc + 1))
        return out

    def exchange_msgs(s, t, phase, part=None):
        reach, q = pad - t, edge(s)
        out = []

        def side(dc, mine, theirs, k, dr=0):
            if part == int(mine[0] == 0):
                return
            src = col_n.at[t, 0 if dc < 0 else 1, pl.ds(mine[0], mine[1] - mine[0])]
            dst = xn.at[t, 1 if dc < 0 else 0, rng(*theirs)]
            out.append((dr, dc, src, dst, k))

        def middle(mine, theirs, k, dr=0):
            if part == int(mine[0] == 0):
                return
            out.append((dr, 0, hc.at[t, rng(*mine)], xc.at[t, rng(*theirs)], k))

        if phase == 0:
            for k, (dr, dc) in enumerate([d for d in DIRS if d[0] and d[1]]):
                mine, theirs = halo(t, reach, dr, dc)
                side(dc, mine, theirs, 8 + k, dr)
            for k, dr in enumerate((-1, 1)):
                mine, theirs = halo(t, reach, dr, 0)
                middle(mine, theirs, 2 + k, dr)
            for k, span in enumerate(((0, q), (rows - q, rows))):
                for j, dc in enumerate((-1, 1)):
                    side(dc, span, span, 4 + 2 * j + k)
            for k, span in enumerate(((0, q), (rows - q, rows))):
                middle(span, span, k)
        else:
            span = (q, rows - q)
            for j, dc in enumerate((-1, 1)):
                side(dc, span, span, 13 + j)
            middle(span, span, 12)
        return out

    def direct_msgs(s, t, phase):
        e, q = extra(s, t), edge(s)
        spans = ((-e, q), (rows - q, rows + e)) if phase == 0 else ((q, rows - q),)
        out = []
        for k, span in enumerate(spans):
            at = rng(*span)
            out.append((0, 0, hc.at[t, at], xc.at[t, at], 6 * phase + 2 * k))
            out.append((0, 0, hr.at[t, at], xe.at[t, 0, at], 6 * phase + 2 * k + 1))
        return out

    def msgs(s, t, phase):
        return direct_msgs(s, t, phase) if direct(s) else exchange_msgs(s, t, phase)

    def each(items, ds, t, sem, act):
        for dr, dc, src, dst, k in items:
            def go(dr=dr, dc=dc, src=src, dst=dst, k=k):
                if act == "recv":
                    pltpu.make_async_remote_copy(
                        src_ref=dst, dst_ref=dst, send_sem=sem.at[t, k], recv_sem=recv_sem.at[t, k],
                        device_id=device(-ds, -dr, -dc), device_id_type=MESH,
                    ).wait_recv()
                    return
                copy = pltpu.make_async_remote_copy(
                    src_ref=src, dst_ref=dst, send_sem=sem.at[t, k], recv_sem=recv_sem.at[t, k],
                    device_id=device(ds, dr, dc), device_id_type=MESH,
                )
                copy.start() if act == "start" else copy.wait_send()
            if (dr, dc) == (0, 0):
                go()
            else:
                pl.when(there(-dr, -dc) if act == "recv" else there(dr, dc))(go)

    barrier = pltpu.get_barrier_semaphore()

    def signal(ds, dr, dc):
        def go():
            pl.semaphore_signal(barrier, inc=1, device_id=device(ds, dr, dc), device_id_type=MESH)
        if (dr, dc) == (0, 0):
            go()
        else:
            pl.when(there(dr, dc))(go)

    def extent(pos, count):
        return 1 + jnp.where(pos > 0, 1, 0) + jnp.where(pos < count - 1, 1, 0)

    near = extent(row, nrow) * extent(col, ncol)

    place = lax.broadcasted_iota(jnp.int32, (RING, width), 0)
    left = jnp.where(col > 0, 1.0, 0.0)
    right = jnp.where(col < ncol - 1, 1.0, 0.0)
    inside = jnp.where(place < RING // 2, right, left)
    above = jnp.where(row > 0, 1.0, 0.0)
    below = jnp.where(row < nrow - 1, 1.0, 0.0)

    def spread(shift, ring, r, line):
        back, ahead = pltpu.roll(line, 1, 0), pltpu.roll(line, wide - 1, 0)
        shift[r + pad, :, 0:width] = back[:cols].astype(bf16)
        shift[r + pad, :, width:] = ahead[:cols].astype(bf16)
        for k, v in enumerate((back, line, ahead)):
            ring[(r + pad) * RING:(r + pad + 1) * RING, k * width:(k + 1) * width] = v[cols:]

    def taps(center, shift, ring, pieces, has_ring, which):
        blocks = []
        for k in which:
            dr, dc = k // 3 - 1, k % 3 - 1
            parts = []
            for r0, n in pieces:
                at = slice(r0 + dr + pad, r0 + dr + pad + n)
                v = center[at] if dc == 0 else shift[at, :, 0:width] if dc < 0 else shift[at, :, width:]
                parts.append(v.reshape(n * cols, width))
            if has_ring:
                lines = [ring[(r0 + dr + pad) * RING:(r0 + dr + pad + n) * RING, (dc + 1) * width:(dc + 2) * width]
                         for r0, n in pieces]
                parts.append((jnp.concatenate(lines, axis=0) if len(lines) > 1 else lines[0]).astype(bf16))
            blocks.append(jnp.concatenate(parts, axis=0) if len(parts) > 1 else parts[0])
        return blocks

    def kernel_of(half, which):
        return [w[k, half * width:(half + 1) * width, :] for k in which]

    def dot(a, b):
        return jnp.dot(jnp.concatenate(a, axis=1), jnp.concatenate(b, axis=0), preferred_element_type=f32)

    every = list(range(9))

    def waits(s, t, c):
        if s == nsec - 1:
            return t == steps - 1 or c == 1
        return not direct(s) and t == steps - 1 and c == 1

    def send_frame(t):
        load_side(t, 0).wait()
        load_side(t, 1).wait()
        load_frame(t).wait()
        each(frame_msgs(t), 0, t, frame_sem, "start")

    def section(s):
        last_sec = s == nsec - 1
        q = edge(s)

        if s == 0:
            for t in range(steps):
                load_side(t, 0).start()
                load_side(t, 1).start()
                load_frame(t).start()
        load_w(0).start()
        load_b.start()
        load_w(1).start()
        if direct(s):
            for t in range(steps):
                xc[t, 0:pad] = jnp.zeros((pad, cols, width), bf16)
                xc[t, pad + rows:] = jnp.zeros((pad, cols, width), bf16)
                if s == 0:
                    xe[t] = jnp.zeros(xe.shape[1:], bf16)
                else:
                    xn[t] = jnp.zeros(xn.shape[1:], bf16)
        if s == 0:
            for dr, dc in DIRS:
                signal(0, dr, dc)
        elif direct(s - 1):
            signal(-1, 0, 0)
        else:
            for dr, dc in [(0, 0)] + DIRS:
                signal(-1, dr, dc)
        wanted = 0
        if s == 0:
            wanted = near - 1
        if not last_sec:
            wanted = wanted + (1 if direct(s) else near)
        if s == 0 or not last_sec:
            pl.semaphore_wait(barrier, wanted)
        if s == 0:
            send_frame(0)
            each(frame_msgs(0), 0, 0, frame_sem, "wait")
            if steps > 1:
                send_frame(1)

        for t in range(steps):
            e = extra(s, t)
            has_ring = e > 0
            span = wide if has_ring else cols
            final = t == steps - 1
            chunks = [[(-e, q + e), (rows - q, q + e)], [(q, rows - 2 * q)]]
            fresh = [[(-e - 1, q + 1), (rows - q - 1, rows + e + 1)], [(q + 1, rows - q - 1)]]
            if t == 1:
                load_w(1).wait()
            for c in range(2):
                pieces = chunks[c]
                split = t > 0 and s > 0 and waits(s, t, c)
                total = sum(n for _, n in pieces)
                if split:
                    acc[0:total * span] = dot(
                        taps(hc.at[t - 1], sh.at[t - 1], rh.at[t - 1], pieces, has_ring, every[:8]),
                        kernel_of(1, every[:8]))
                if s > 0:
                    each(msgs(s - 1, t, c), 1, t, send_sem, "recv")
                elif c == 0:
                    each(frame_msgs(t), 0, t, frame_sem, "recv")
                    if t + 2 < steps:
                        send_frame(t + 2)
                for lo, hi in fresh[c]:
                    for r in range(lo, hi):
                        if direct(s) and s > 0:
                            ring = jnp.concatenate([xn[t, 1, r + pad].astype(f32), xn[t, 0, r + pad].astype(f32)], axis=0)
                        elif direct(s):
                            ring = jnp.where(place < RING // 2, xe[t, 1, r + pad].astype(f32), xe[t, 0, r + pad].astype(f32))
                        else:
                            ring = xe[t, 0, r + pad].astype(f32)
                        spread(sx, rx, r, jnp.concatenate([xc[t, r + pad].astype(f32), ring], axis=0))
                if t == 0 and c == 0:
                    load_w(0).wait()
                    load_b.wait()
                blocks = [[p] for p in pieces] if c == 0 and not last_sec and not direct(s) else [pieces]
                for i, part in enumerate(blocks):
                    a = taps(xc.at[t], sx, rx, part, has_ring, every)
                    b = kernel_of(0, every)
                    if t > 0:
                        which = every[8:] if split else every
                        a = a + taps(hc.at[t - 1], sh.at[t - 1], rh.at[t - 1], part, has_ring, which)
                        b = b + kernel_of(1, which)
                    pre = dot(a, b) + bias[...]
                    if split:
                        pre = pre + acc[0:total * span]
                    at_core, at_ring = 0, sum(n for _, n in part) * cols
                    for r0, n in part:
                        groups = [(cols, at_core, cell_c)] + ([(RING, at_ring, cell_r)] if has_ring else [])
                        made = []
                        for span_g, at, mem in groups:
                            p = pre[at:at + n * span_g]
                            shape = (n, span_g, width)
                            added = (sigmoid(p[:, :width]) * jnp.tanh(p[:, 2 * width:3 * width])).reshape(shape)
                            cell = added
                            if t > 0:
                                kept = sigmoid(p[:, width:2 * width]).reshape(shape) * mem[r0 + pad:r0 + pad + n]
                                cell = kept + added
                            opened = sigmoid(p[:, 3 * width:]).reshape(shape)
                            if not final:
                                mem[r0 + pad:r0 + pad + n] = cell
                            elif span_g == cols:
                                lo, hi = max(r0, 0), min(r0 + n, rows)
                                kept_out[0, lo:hi] = kept[lo - r0:hi - r0]
                                added_out[0, lo:hi] = added[lo - r0:hi - r0]
                                gate_out[0, lo:hi] = opened[lo - r0:hi - r0]
                            made.append(opened * jnp.tanh(cell))
                        at_core, at_ring = at_core + n * cols, at_ring + n * RING
                        if final and last_sec:
                            continue
                        for r in range(r0, r0 + n):
                            core = made[0][r - r0]
                            if has_ring:
                                ring = made[1][r - r0] * inside
                            if r < 0:
                                core, ring = core * above, ring * above
                            elif r >= rows:
                                core, ring = core * below, ring * below
                            hc[t, r + pad] = core.astype(bf16)
                            if not last_sec:
                                if direct(s):
                                    hr[t, r + pad] = ring.astype(bf16)
                                elif 0 <= r < rows:
                                    col_n[t, 0, r] = core[:RING // 2].astype(bf16)
                                    col_n[t, 1, r] = core[cols - RING // 2:].astype(bf16)
                            if not final:
                                spread(sh.at[t], rh.at[t], r, jnp.concatenate([core, ring], axis=0))
                    if len(blocks) > 1:
                        each(exchange_msgs(s, t, c, i), 1, t, send_sem, "start")
                    elif not last_sec:
                        each(msgs(s, t, c), 1, t, send_sem, "start")

        if s == 0:
            for t in range(1, steps):
                each(frame_msgs(t), 0, t, frame_sem, "wait")
        if steps == 1:
            load_w(1).wait()
        if not last_sec:
            for t in range(steps):
                for c in range(2):
                    each(msgs(s, t, c), 1, t, send_sem, "wait")

    for s in range(nsec):
        @pl.when(sec == s)
        def _(s=s):
            section(s)


def solution(mesh):
    sizes = (mesh.shape["section"], mesh.shape["row"], mesh.shape["col"])

    def step(frames, weight, bias):
        steps, rows, cols, width = frames.shape
        pad = steps + 1
        assert pad <= RING // 2 and 2 * (sizes[0] + 1) < rows
        high = rows + 2 * pad
        vmem = pl.BlockSpec(memory_space=pltpu.VMEM)
        hbm = pl.BlockSpec(memory_space=pl.ANY)
        bf16, f32 = jnp.bfloat16, jnp.float32
        kept, added, opened = pl.pallas_call(
            lambda *refs: body(sizes, *refs),
            out_shape=(jax.ShapeDtypeStruct((1, rows, cols, width), f32),) * 3,
            in_specs=[hbm, hbm, hbm],
            out_specs=(vmem, vmem, vmem),
            scratch_shapes=[
                pltpu.VMEM((steps, high, cols, width), bf16),
                pltpu.VMEM((steps, 2, high, RING, width), bf16),
                pltpu.VMEM((steps, 2, high, RING // 2, width), bf16),
                pltpu.VMEM((steps, high, cols, width), bf16),
                pltpu.VMEM((steps, high, RING, width), bf16),
                pltpu.VMEM((steps, 2, rows, RING, width), bf16),
                pltpu.VMEM((steps, 2, rows, RING // 2, width), bf16),
                pltpu.VMEM(weight.shape[1:], bf16),
                pltpu.VMEM(bias.shape, f32),
                pltpu.VMEM((high, cols, 2 * width), bf16),
                pltpu.VMEM((high * RING, 3 * width), f32),
                pltpu.VMEM((steps, high, cols, 2 * width), bf16),
                pltpu.VMEM((steps, high * RING, 3 * width), f32),
                pltpu.VMEM((high * (cols + RING), 4 * width), f32),
                pltpu.VMEM((high, cols, width), f32),
                pltpu.VMEM((high, RING, width), f32),
                pltpu.SemaphoreType.DMA((3 * steps + 3,)),
                pltpu.SemaphoreType.DMA((steps, MSGS)),
                pltpu.SemaphoreType.DMA((steps, MSGS)),
                pltpu.SemaphoreType.DMA((steps, MSGS)),
            ],
            compiler_params=pltpu.CompilerParams(
                collective_id=0, has_side_effects=True, vmem_limit_bytes=24 << 20),
        )(*[pltpu.with_memory_space_constraint(v, pltpu.HBM) for v in (frames, weight, bias)])
        cell = kept + added
        return (opened * jnp.tanh(cell)).astype(bf16), cell

    return jax.shard_map(
        step,
        mesh=mesh,
        in_specs=(P(None, "row", "col", None), P("section", None, None, None), P("section", None)),
        out_specs=(P("section", "row", "col", None), P("section", "row", "col", None)),
        check_vma=False,
    )
```
